32 devices in a mesh: up: 4 (over y, x), dn: 8 (over z, core).
Axes of the slice: x: 2, y: 2, z: 4, core: 2. Of those that a mesh axis runs over, the one named last changes fastest.
Arguments:
- coefficients: float32 [16384, 8192], P('up', 'dn'), may hold values from -6 to 6
- hopping_up: float32 [8, 128, 128], replicated, may hold values from -0.375 to 0.375
- partner_bits_up: int32 [7], replicated, may hold values from 0 to 6, each once
- block_signs_up: int32 [7, 128], replicated, may hold values from -2 to 2
- hopping_down: float32 [7, 128, 128], replicated, may hold values from -0.375 to 0.375
- partner_bits_down: int32 [6], replicated, may hold values from 0 to 5, each once
- block_signs_down: int32 [6, 64], replicated, may hold values from -2 to 2
- occupied_up: int32 [14, 16384], P(None, 'up'), may hold values 0 or 1
- occupied_down: int32 [14, 8192], P(None, 'dn'), may hold values 0 or 1
- site_energy: float32 [14], replicated, may hold values from 0.1 to 0.5
- repulsion: float32 [14], replicated, may hold values from 0.25 to 1
- energy_shift: float32 [], replicated, may hold values from -3 to -1
Outputs:
- residual: float32 [16384, 8192], P('up', 'dn')
- updated: float32 [16384, 8192], P('up', 'dn')
The draws below stay inside these ranges and needn't reach their ends.
Inputs may be any that keep to these rules, and one draw needn't show every extreme that they name: `partner_bits_up`: each bit number of an up block appears exactly once. `partner_bits_down`: each bit number of a down block appears exactly once.
All inputs are finite; a program needn't handle non-finite values. No bound on the sum of `occupied_up` or of `occupied_down` on one device may be relied on, other than what follows from the above.
Results may differ from the reference program's by a relative error of at most 0.0001.
Values sent between devices are 32-bit elements; how exact they have to be, the bound alone decides.
A program may use at most 448 MiB of HBM per device.

```python
import math
import jax
import jax.numpy as jnp
from jax import lax

BLK = 128
ABITS = 7
DBITS = 6
SITES = 14
NA = 16384
NB = 8192


def touch_ends(entries, key, smallest, top_value):
    index_at = [jax.random.randint(jax.random.fold_in(key, axis), (), 0, length) for axis, length in enumerate(entries.shape)]
    widest = entries.shape.index(max(entries.shape))
    neighbour = index_at[:widest] + [(index_at[widest] + 1) % entries.shape[widest]] + index_at[widest + 1:]
    return entries.at[tuple(index_at)].set(smallest).at[tuple(neighbour)].set(top_value)


def level_of(rng, extent, shards, low, high):
    level, own = 1.0, jax.random.fold_in(rng, 6)
    for position, blocks in shards:
        heights = jnp.exp(jax.random.uniform(jax.random.fold_in(own, position), (blocks,), jnp.float32, low / len(shards), high / len(shards)))
        level = level * jnp.repeat(heights, extent[position] // blocks).reshape([-1 if axis == position else 1 for axis in range(len(extent))])
    return level


def bell_draw(rng, shape, spread, most, split=(), held_as=jnp.bfloat16):
    gain = level_of(rng, shape, split, -0.22, 0.18) if split else 1.0
    values = jax.random.normal(rng, shape, jnp.float32) * spread * gain
    return jnp.minimum(jnp.maximum(values, -most), most).astype(held_as)


def setup_inputs(seed: int = 0) -> dict:
    streams_of = jax.random.split(jax.random.key(seed), 13)
    coefficients = bell_draw(streams_of[0], (NA, NB), 1.0, 6.0, ((0, 4), (1, 8)), jnp.float32)
    hopping_up = bell_draw(streams_of[1], (ABITS + 1, BLK, BLK), (2 * BLK) ** -0.5, 0.375, (), jnp.float32)
    partner_bits_up = jax.random.permutation(streams_of[2], ABITS).astype(jnp.int32)
    block_signs_up = touch_ends(jax.random.randint(streams_of[3], (ABITS, NA // BLK), -2, 3), jax.random.fold_in(streams_of[3], 1), -2, 2).astype(jnp.int32)
    hopping_down = bell_draw(streams_of[4], (DBITS + 1, BLK, BLK), (2 * BLK) ** -0.5, 0.375, (), jnp.float32)
    partner_bits_down = jax.random.permutation(streams_of[5], DBITS).astype(jnp.int32)
    block_signs_down = touch_ends(jax.random.randint(streams_of[6], (DBITS, NB // BLK), -2, 3), jax.random.fold_in(streams_of[6], 1), -2, 2).astype(jnp.int32)
    occupied_up = touch_ends((jax.random.randint(streams_of[7], (SITES, NA), 0, 2) < 1).astype(jnp.int32), jax.random.fold_in(streams_of[7], 1), 0, 1)
    occupied_down = touch_ends((jax.random.randint(streams_of[8], (SITES, NB), 0, 2) < 1).astype(jnp.int32), jax.random.fold_in(streams_of[8], 1), 0, 1)
    site_energy = jnp.clip(jnp.exp(jax.random.uniform(streams_of[9], (SITES,), jnp.float32, math.log(0.1), math.log(0.5))), 0.1, 0.5)
    repulsion = jnp.clip(jnp.exp(jax.random.uniform(streams_of[10], (SITES,), jnp.float32, math.log(0.25), math.log(1.0))), 0.25, 1.0)
    energy_shift = jnp.clip(jax.random.uniform(streams_of[11], (), jnp.float32, -3.0, -1.0), -3.0, -1.0)
    return {"coefficients": coefficients, "hopping_up": hopping_up, "partner_bits_up": partner_bits_up, "block_signs_up": block_signs_up, "hopping_down": hopping_down, "partner_bits_down": partner_bits_down, "block_signs_down": block_signs_down, "occupied_up": occupied_up, "occupied_down": occupied_down, "site_energy": site_energy, "repulsion": repulsion, "energy_shift": energy_shift}


def hop_blocks(blocks, hopping, partner_bits, block_signs):
    block_count = blocks.shape[0]
    result = jnp.einsum("ij,pjw->piw", hopping[0], blocks, precision=lax.Precision.HIGHEST)
    numbers = jnp.arange(block_count, dtype=jnp.int32)
    for term_index in range(hopping.shape[0] - 1):
        flipper = jnp.left_shift(jnp.int32(1), partner_bits[term_index].astype(jnp.int32)).astype(jnp.int32)
        partner = jnp.bitwise_xor(numbers, flipper).astype(jnp.int32)
        moved = blocks[partner]
        product = jnp.einsum("ij,pjw->piw", hopping[term_index + 1], moved, precision=lax.Precision.HIGHEST)
        result = result + block_signs[term_index].astype(jnp.float32)[:, None, None] * product
    return result


def reference(coefficients, hopping_up, partner_bits_up, block_signs_up, hopping_down, partner_bits_down, block_signs_down, occupied_up, occupied_down, site_energy, repulsion, energy_shift):
    row_count, col_count = coefficients.shape
    up_blocks = coefficients.reshape(row_count // BLK, BLK, col_count)
    up_term = hop_blocks(up_blocks, hopping_up, partner_bits_up, block_signs_up).reshape(row_count, col_count)
    down_blocks = coefficients.T.reshape(col_count // BLK, BLK, row_count)
    down_term = hop_blocks(down_blocks, hopping_down, partner_bits_down, block_signs_down).reshape(col_count, row_count).T
    occ_up_f = occupied_up.astype(jnp.float32)
    occ_down_f = occupied_down.astype(jnp.float32)
    energy_up = jnp.dot(site_energy, occ_up_f, precision=lax.Precision.HIGHEST)
    energy_down = jnp.dot(site_energy, occ_down_f, precision=lax.Precision.HIGHEST)
    scaled_up = repulsion[:, None] * occ_up_f
    interaction = jnp.dot(scaled_up.T, occ_down_f, precision=lax.Precision.HIGHEST)
    diagonal = energy_up[:, None] + energy_down[None, :] + interaction
    sigma = up_term + down_term + diagonal * coefficients
    residual = sigma - energy_shift * coefficients
    updated = coefficients - residual / (diagonal - energy_shift)
    return residual, updated
```

```python
import functools

import jax
import jax.numpy as jnp
from jax import lax
from jax.experimental import pallas as pl
from jax.experimental.pallas import tpu as pltpu
from jax.sharding import PartitionSpec as P


PARAMS = pltpu.CompilerParams(vmem_limit_bytes=60 * 1024 * 1024)
SMEM = pl.BlockSpec(memory_space=pltpu.SMEM)
WHOLE = pl.BlockSpec(memory_space=pltpu.VMEM)


def swapped(x, axis, apart):
    return lax.ppermute(x, axis, [(i, i ^ 1 << apart) for i in range(lax.axis_size(axis))])


def dot(a, b):
    return jnp.dot(a, b, precision=lax.Precision.HIGHEST, preferred_element_type=jnp.float32)


def by_bit(hopping, partner_bits, block_signs, first_block, block_count):
    bits = hopping.shape[0] - 1
    order = jnp.argsort(partner_bits)
    matrices = jnp.concatenate([hopping[:1], hopping[1:][order]])
    signs = lax.dynamic_slice_in_dim(block_signs[order], first_block, block_count, axis=1)
    ones = jnp.ones((1, block_count), jnp.float32)
    assert matrices.shape[0] == bits + 1
    return matrices, jnp.concatenate([ones, signs.astype(jnp.float32)])


def up_kernel(bits, signs, hop, values, out):
    size = hop.shape[1]

    def block(p, _):
        total = None
        for k in range(bits + 1):
            partner = p if k == 0 else p ^ (1 << (k - 1))
            rows = pl.ds(pl.multiple_of(partner * size, size), size)
            term = dot(hop[k] * signs[k, p], values[rows, :])
            total = term if total is None else total + term
        out[pl.ds(pl.multiple_of(p * size, size), size), :] = total
        return 0

    lax.fori_loop(0, values.shape[0] // size, block, 0)


def row_kernel(up_bits, up_far, down_bits, down_near, signs_up, signs_down, hop_up, hop_down, partial, values, *rest):
    ups, downs, out = rest[:up_far], rest[up_far:-1], rest[-1]
    size = hop_up.shape[1]
    p = pl.program_id(0)
    count = values.shape[1] // size
    left = [hop_up[up_bits + 1 + f] * signs_up[up_bits + 1 + f, p] for f in range(up_far)]
    for q in range(count):
        at = pl.ds(q * size, size)
        total = partial[:, at]
        for f in range(up_far):
            total = total + dot(left[f], ups[f][:, at])
        for k in range(down_bits + 1):
            partner = q if k == 0 else q ^ (1 << (k - 1))
            total = total + dot(values[:, pl.ds(partner * size, size)], hop_down[k] * signs_down[k, q])
        for f in range(down_near):
            k = down_bits + 1 + f
            total = total + dot(downs[f][:, at], hop_down[k] * signs_down[k, q])
        out[:, at] = total


def last_kernel(first_term, far, chained, signs_down, hop_down, side, top, partial, values, *rest):
    downs = rest[:far]
    residual, updated = rest[-2:]
    size = hop_down.shape[1]
    for q in range(values.shape[1] // size):
        at = pl.ds(q * size, size)
        total = partial[:, at]
        for f in range(far):
            k = first_term + f
            total = total + dot(downs[f][:, at], hop_down[k] * signs_down[k, q])
        gap = dot(side[...], top[:, at])
        own = values[:, at]
        total = total + gap * own
        residual[:, at] = total
        updated[:, at] = own - total / gap


def shards(
    coefficients,
    hopping_up,
    partner_bits_up,
    block_signs_up,
    hopping_down,
    partner_bits_down,
    block_signs_down,
    occupied_up,
    occupied_down,
    site_energy,
    repulsion,
    energy_shift,
):
    row_count, col_count = coefficients.shape
    size = hopping_up.shape[1]
    up_local, down_local = row_count // size, col_count // size
    up_bits, down_bits = up_local.bit_length() - 1, down_local.bit_length() - 1
    up_far = hopping_up.shape[0] - 1 - up_bits
    down_far = hopping_down.shape[0] - 1 - down_bits
    down_near = min(1, down_far)
    slow = down_far - down_near
    whole_bytes = row_count * col_count * 4
    term_flops = 2 * 6 * row_count * col_count * size

    weights = (4, 12, 12, 12, 12, 8, 2, 1, 1)
    unit = row_count // sum(weights)
    sizes = [w * unit for w in weights]
    firsts = [sum(sizes[:i]) for i in range(len(sizes))]

    far_chunks = []
    source = coefficients
    for first, rows in zip(firsts, sizes):
        chunk = lax.slice_in_dim(source, first, first + rows)
        source, chunk = lax.optimization_barrier((source, chunk))
        far_chunks.append([swapped(chunk, "dn", down_near + f) for f in range(slow)])
        if first == 0:
            ups = [swapped(source, "up", f) for f in range(up_far)]
            nears = [swapped(source, "dn", f) for f in range(down_near)]

    hop_up, signs_up = by_bit(
        hopping_up, partner_bits_up, block_signs_up, lax.axis_index("up") * up_local, up_local
    )
    hop_down, signs_down = by_bit(
        hopping_down, partner_bits_down, block_signs_down, lax.axis_index("dn") * down_local, down_local
    )
    hop_down = hop_down.transpose(0, 2, 1)

    occ_up = occupied_up.astype(jnp.float32)
    occ_down = occupied_down.astype(jnp.float32)
    energy_up = jnp.dot(site_energy, occ_up, precision=lax.Precision.HIGHEST)
    energy_down = jnp.dot(site_energy, occ_down, precision=lax.Precision.HIGHEST) - energy_shift
    side = jnp.concatenate([(repulsion[:, None] * occ_up), energy_up[None], jnp.ones_like(energy_up)[None]]).T
    top = jnp.concatenate([occ_down, jnp.ones_like(energy_down)[None], energy_down[None]])
    inner = side.shape[1]

    width = min(2 * size, col_count)
    column_spec = pl.BlockSpec((row_count, width), lambda j: (0, j))
    partial = pl.pallas_call(
        functools.partial(up_kernel, up_bits),
        grid=(col_count // width,),
        in_specs=[SMEM, WHOLE, column_spec],
        out_specs=column_spec,
        out_shape=jax.ShapeDtypeStruct((row_count, col_count), jnp.float32),
        compiler_params=PARAMS,
        cost_estimate=pl.CostEstimate(
            flops=(up_bits + 1) * term_flops, bytes_accessed=2 * whole_bytes, transcendentals=0
        ),
        name="up_local",
    )(signs_up, hop_up, coefficients)

    row_spec = pl.BlockSpec((size, col_count), lambda i: (i, 0))
    partial = pl.pallas_call(
        functools.partial(row_kernel, up_bits, up_far, down_bits, down_near),
        grid=(up_local,),
        in_specs=[SMEM, SMEM, WHOLE, WHOLE] + [row_spec] * (2 + up_far + down_near),
        out_specs=row_spec,
        out_shape=jax.ShapeDtypeStruct((row_count, col_count), jnp.float32),
        compiler_params=PARAMS,
        cost_estimate=pl.CostEstimate(
            flops=(up_far + down_bits + 1 + down_near) * term_flops,
            bytes_accessed=(3 + up_far + down_near) * whole_bytes,
            transcendentals=0,
        ),
        name="rows",
    )(signs_up, signs_down, hop_up, hop_down, partial, coefficients, *ups, *nears)

    results = None
    for first, rows, downs in zip(firsts, sizes, far_chunks):
        tile = min(rows, 4 * unit)
        while first % tile or rows % tile:
            tile -= unit
        start = first // tile
        here = lambda i, start=start: (start + i, 0)
        wide = pl.BlockSpec((tile, col_count), here)
        chunk_spec = pl.BlockSpec((tile, col_count), lambda i: (i, 0))
        operands = [signs_down, hop_down, side, top, partial, coefficients, *downs]
        in_specs = [SMEM, WHOLE, pl.BlockSpec((tile, inner), here), WHOLE, wide, wide] + [chunk_spec] * slow
        aliases = {}
        if results is not None:
            aliases = {len(operands): 0, len(operands) + 1: 1}
            operands += results
            in_specs += [pl.BlockSpec(memory_space=pl.ANY)] * 2
        shape = jax.ShapeDtypeStruct((row_count, col_count), jnp.float32)
        results = pl.pallas_call(
            functools.partial(last_kernel, down_bits + 1 + down_near, slow, results is not None),
            grid=(rows // tile,),
            in_specs=in_specs,
            out_specs=[wide, wide],
            out_shape=[shape, shape],
            input_output_aliases=aliases,
            compiler_params=PARAMS,
            cost_estimate=pl.CostEstimate(
                flops=(slow + 1) * term_flops * rows // row_count,
                bytes_accessed=(4 + slow) * whole_bytes * rows // row_count,
                transcendentals=0,
            ),
            name="finish",
        )(*operands)
    return tuple(results)


def solution(mesh):
    placed = (
        P("up", "dn"),
        P(),
        P(),
        P(),
        P(),
        P(),
        P(),
        P(None, "up"),
        P(None, "dn"),
        P(),
        P(),
        P(),
    )
    return jax.shard_map(
        shards,
        mesh=mesh,
        in_specs=placed,
        out_specs=(P("up", "dn"), P("up", "dn")),
        check_vma=False,
    )
```
